32 devices in a mesh: section: 4 (over x, core), expert: 8 (over z, y).
Axes of the slice: x: 2, y: 2, z: 4, core: 2. Of those that a mesh axis runs over, the one named last changes fastest.
Arguments:
- tokens: bfloat16 [2048, 7168], P('expert', 'section'), may hold values from -6 to 6
- gate_up: bfloat16 [8, 7168, 2, 1024], P('expert', 'section'), may hold values from -0.0625 to 0.0625
- down_weight: bfloat16 [8, 1024, 7168], P('expert', None, 'section'), may hold values from -0.1875 to 0.1875
- expert_ids: int32 [2048, 8], P('expert'), may hold values from 0 to 31, all different within a row; in each aligned block of 256 rows (0 to 255, 256 to 511, ...) at most 96 rows name the same one
- gate_values: float32 [2048, 8], P('expert'), may hold values from 0.2 to 1
- owner_map: int32 [8], replicated, may hold values from 0 to 7, each once
Outputs:
- mixed: bfloat16 [2048, 7168], P('expert', 'section')
The draws below stay inside these ranges and needn't reach their ends.
Inputs may be any that keep to these rules, and one draw needn't show every extreme that they name: `expert_ids`: each row names 8 different experts; among the 256 rows of one index of expert no expert is named more than 96 times. `owner_map`: each owner holds exactly one expert.
All inputs are finite; a program needn't handle non-finite values.
Results may differ from the reference program's by a relative error of at most 0.028.
Values may be sent and summed in bfloat16 or wider, within the bound.
A program may use at most 64 MiB of HBM per device.

```python
import math
import jax
import jax.numpy as jnp
import numpy as np
from jax import lax

D = 7168
FF = 1024
TOP = 8
TOK_DEV = 256
ROUTED = 32
EXPERTS = 8
CAP = 96
D_DEV = 1792
TOKENS = 2048
N_SECTION = 4
N_EXPERT = 8


def block_levels(stream_key, extent, pieces, least, high):
    def one(dim, shards_of):
        steps = jax.random.uniform(jax.random.fold_in(jax.random.fold_in(stream_key, 6), dim), (shards_of,), jnp.float32, least / len(pieces), high / len(pieces))
        return jnp.repeat(jnp.exp(steps), extent[dim] // shards_of).reshape((-1,) + (1,) * (len(extent) - dim - 1))

    factor_of = one(*pieces[0])
    for cut in pieces[1:]:
        factor_of = factor_of * one(*cut)
    return factor_of


def deal_out(key, own, number, rows, amount, top, bound, slope):
    sequence = jax.random.permutation(key, amount)
    packed, ordinary = load_shares(amount, rows * top, bound, slope, True), load_shares(amount, rows * top, bound, slope, False)
    places = jnp.arange(amount)

    def named(tallies, rotation):
        used = int((tallies > 0).sum())
        fixed = max(1, used // 4)
        moved = fixed + (places - fixed + rotation * (used - fixed)) % max(1, amount - fixed)
        return jnp.zeros((amount,), jnp.int32).at[sequence[jnp.where(places < fixed, places, moved)]].set(jnp.asarray(tallies, jnp.int32))

    tallies = jnp.where(number % 4 == 0, named(packed, number // 4), named(ordinary, number - number // 4 - 1))
    mixed = jax.random.permutation(jax.random.fold_in(own, 3), amount)
    giver, sink = mixed[0:amount // 2 * 2:2], mixed[1:amount // 2 * 2:2]
    slack = jnp.minimum(tallies[giver] - 1, bound - tallies[sink]) // 2
    slack = jnp.where((giver == sequence[0]) | (sink == sequence[0]) | (tallies[sink] == 0), 0, jnp.maximum(slack, 0))
    moved = jax.random.randint(jax.random.fold_in(own, 4), (amount // 2,), 0, 1 << 20) % (slack + 1)
    tallies = tallies.at[giver].add(-moved).at[sink].add(moved)
    labels = jnp.searchsorted(jnp.cumsum(tallies), jnp.arange(rows * top), side="right").astype(jnp.int32)
    grid = labels.reshape(top, rows).T
    grid = grid[jax.random.permutation(jax.random.fold_in(own, 1), rows)]
    rotation = jax.random.randint(jax.random.fold_in(own, 2), (rows, 1), 0, top)
    return jnp.take_along_axis(grid, (jnp.arange(top)[None, :] + rotation) % top, axis=1)


def load_shares(number_of, total, limit, skew, full):
    weights = [(1 << 20) // math.isqrt(grade ** skew) + 1 for grade in range(1, number_of + 1)]
    largest = limit if full else min(limit, max(-(-total // number_of), total * weights[0] // sum(weights)))
    least = 1 if total - largest >= number_of - 1 else 0
    holding, surplus = [largest] + [least] * (number_of - 1), total - largest - least * (number_of - 1)
    while surplus > 0:
        movable = [i for i in range(1, number_of) if holding[i] < largest] or [i for i in range(1, number_of) if holding[i] < limit]
        mass, remaining = sum([weights[i] for i in movable]), surplus
        for i in movable:
            extra = min(limit - holding[i], max(1, remaining * weights[i] // mass), surplus)
            holding[i] = holding[i] + extra
            surplus = surplus - extra
    return np.array(holding)


def scatter_about(key, extent, width, most, cuts=(), held_as=jnp.bfloat16):
    factor_of = block_levels(key, extent, cuts, -0.22, 0.18) if cuts else 1.0
    drawn = jax.random.normal(key, extent, jnp.float32) * width * factor_of
    return jnp.minimum(jnp.maximum(drawn, -most), most).astype(held_as)


def setup_inputs(seed: int = 0) -> dict:
    arg_keys = jax.random.split(jax.random.key(seed), 7)
    tokens = scatter_about(arg_keys[0], (TOKENS, D), 1.0, 6.0, ((0, 8), (1, 4)))
    gate_up = scatter_about(arg_keys[1], (EXPERTS, D, 2, FF), D ** -0.5, 0.0625, ((0, 8), (1, 4)))
    down_weight = scatter_about(arg_keys[2], (EXPERTS, FF, D), FF ** -0.5, 0.1875, ((0, 8), (2, 4)))
    expert_ids_keys = jax.random.split(jax.random.fold_in(arg_keys[3], 1), TOKENS // TOK_DEV)
    expert_ids_turns = jax.random.permutation(jax.random.fold_in(arg_keys[3], 3), TOKENS // TOK_DEV)
    expert_ids = jax.vmap(lambda own, number: deal_out(jax.random.fold_in(arg_keys[3], 2), own, number, TOK_DEV, ROUTED, TOP, CAP, 1))(expert_ids_keys, expert_ids_turns).reshape((TOKENS, TOP))
    gate_values = jnp.clip(jnp.exp(math.log(1.0) - 1.609438 * jax.random.uniform(arg_keys[4], (TOKENS, TOP), jnp.float32) ** block_levels(arg_keys[4], (TOKENS, TOP), ((0, 8),), -0.2, 0.2)), 0.2, 1.0)
    owner_map = jax.random.permutation(arg_keys[5], EXPERTS).astype(jnp.int32)
    return {"tokens": tokens, "gate_up": gate_up, "down_weight": down_weight, "expert_ids": expert_ids, "gate_values": gate_values, "owner_map": owner_map}


def expert_pass(tokens, gate_up, down_weight, expert_ids, gate_values, owner_map, index):
    hits = expert_ids == index
    chosen = jnp.any(hits, axis=1)
    weight_sum = jnp.sum(jnp.where(hits, gate_values, jnp.float32(0.0)), axis=1)
    blocked = chosen.reshape(N_EXPERT, TOK_DEV).astype(jnp.int32)
    ranks = jnp.cumsum(blocked, axis=1).astype(jnp.int32) - 1
    slots = jnp.arange(N_EXPERT, dtype=jnp.int32)[:, None] * CAP + ranks
    slots = jnp.where(blocked > 0, slots, N_EXPERT * CAP).reshape(-1).astype(jnp.int32)
    row_index = jnp.zeros((N_EXPERT * CAP + 1,), jnp.int32).at[slots].set(jnp.arange(TOKENS, dtype=jnp.int32))[:-1]
    slot_weight = jnp.zeros((N_EXPERT * CAP + 1,), jnp.float32).at[slots].set(weight_sum)[:-1]
    rows = tokens[row_index]
    place = owner_map[index]
    weight_in = lax.dynamic_index_in_dim(gate_up, place, 0, keepdims=False)
    weight_out = lax.dynamic_index_in_dim(down_weight, place, 0, keepdims=False)
    count = rows.shape[0]
    split_rows = rows.astype(jnp.float32).reshape(count, N_SECTION, D_DEV)
    split_weight = weight_in.astype(jnp.float32).reshape(N_SECTION, D_DEV, 2 * FF)
    partial_sums = jnp.einsum('rsd,sdf->srf', split_rows, split_weight, precision=lax.Precision.HIGHEST)
    rounded = lax.optimization_barrier(partial_sums.astype(jnp.bfloat16))
    projected = jnp.sum(rounded.astype(jnp.float32), axis=0)
    hidden = (jax.nn.silu(projected[:, :FF]) * projected[:, FF:]).astype(jnp.bfloat16)
    expert_out = jnp.dot(hidden, weight_out, preferred_element_type=jnp.float32).astype(jnp.bfloat16)
    return row_index, slot_weight[:, None] * expert_out.astype(jnp.float32)


def reference(tokens, gate_up, down_weight, expert_ids, gate_values, owner_map):
    def step_fn(total, index):
        row_index, contrib = expert_pass(tokens, gate_up, down_weight, expert_ids, gate_values, owner_map, index)
        return total.at[row_index].add(contrib), None

    start = jnp.zeros((TOKENS, D), jnp.float32)
    total, unused = lax.scan(step_fn, start, jnp.arange(EXPERTS, dtype=jnp.int32))
    return total.astype(jnp.bfloat16)
```

```python
import functools

import jax
import jax.numpy as jnp
from jax import lax
from jax.experimental import pallas as pl
from jax.experimental.pallas import tpu as pltpu
from jax.sharding import PartitionSpec as P

MESH = pl.DeviceIdType.MESH
F32, BF16 = jnp.float32, jnp.bfloat16


def partner(me, k, n):
    out, bit = me, 1
    while bit < n:
        out = out + ((k // bit) % 2) * (1 - 2 * ((me // bit) % 2)) * bit
        bit *= 2
    return out


def layer_kernel(
    n, q,
    tok, code, wts, win_hbm, wout_hbm, out,
    win, wout, send, recv, psend, precv, hid, osend, back, acc,
    wsem, asend, arecv, bsend, brecv, csend, crecv, dsend, drecv,
):
    me = lax.axis_index("expert")
    sec = lax.axis_index("section")
    slots, width = send.shape[1], send.shape[2]
    rows = tok.shape[0]
    cols = hid.shape[3]

    load_in = pltpu.make_async_copy(win_hbm, win, wsem.at[0])
    load_out = pltpu.make_async_copy(wout_hbm, wout, wsem.at[1])
    load_in.start()
    load_out.start()

    barrier = pltpu.get_barrier_semaphore()

    def greet(k, c):
        pl.semaphore_signal(barrier, inc=1, device_id={"expert": partner(me, k, n)}, device_id_type=MESH)
        return c

    lax.fori_loop(1, n, greet, 0)
    for r in range(1, q):
        pl.semaphore_signal(barrier, inc=1, device_id={"section": (sec + r) % q}, device_id_type=MESH)
    pl.semaphore_wait(barrier, n + q - 2)

    slot_iota = lax.broadcasted_iota(jnp.int32, (slots, rows), 0)

    def a_copy(k):
        return pltpu.make_async_remote_copy(
            src_ref=send.at[k], dst_ref=recv.at[k], send_sem=asend.at[k], recv_sem=arecv.at[k],
            device_id={"expert": partner(me, k, n)}, device_id_type=MESH)

    def d_copy(k):
        return pltpu.make_async_remote_copy(
            src_ref=osend.at[k], dst_ref=back.at[k], send_sem=dsend.at[k], recv_sem=drecv.at[k],
            device_id={"expert": partner(me, k, n)}, device_id_type=MESH)

    def pick(k):
        hot = (code[partner(me, k, n)] == slot_iota).astype(F32).astype(BF16)
        return jnp.dot(hot, tok[...], preferred_element_type=F32).astype(BF16)

    def dispatch(i, c):
        k = n - i
        send[k] = pick(k)
        a_copy(k).start()
        return c

    lax.fori_loop(1, n, dispatch, 0)
    recv[0] = pick(0)
    load_in.wait()
    load_out.wait()

    def project(k):
        @pl.when(k != 0)
        def _():
            a_copy(k).wait_recv()

        for step in range(q):
            r = (step + 1) % q
            j = (sec + r) % q
            at = pl.ds(pl.multiple_of(j * cols, cols), cols)
            for g in range(2):
                part = jnp.dot(recv[k], win[g, :, at], preferred_element_type=F32)
                psend[k, r, :, g * cols:(g + 1) * cols] = part.astype(BF16)
            if r:
                pltpu.make_async_remote_copy(
                    src_ref=psend.at[k, r], dst_ref=precv.at[k, r - 1],
                    send_sem=bsend.at[k], recv_sem=brecv.at[k],
                    device_id={"section": j}, device_id_type=MESH).start()

    def b_all(k):
        return pltpu.make_async_remote_copy(
            src_ref=psend.at[k, pl.ds(1, q - 1)], dst_ref=precv.at[k],
            send_sem=bsend.at[k], recv_sem=brecv.at[k],
            device_id={"section": (sec + 1) % q}, device_id_type=MESH)

    def activate(k):
        b_all(k).wait_recv()
        total = psend[k, 0].astype(F32)
        for r in range(q - 1):
            total = total + precv[k, r].astype(F32)
        gate, up = total[:, :cols], total[:, cols:]
        hid[k, sec] = (gate / (1.0 + jnp.exp(-gate)) * up).astype(BF16)
        for r in range(1, q):
            pltpu.make_async_remote_copy(
                src_ref=hid.at[k, sec], dst_ref=hid.at[k, sec],
                send_sem=csend.at[k], recv_sem=crecv.at[k],
                device_id={"section": (sec + r) % q}, device_id_type=MESH).start()

    def c_all(k):
        return pltpu.make_async_remote_copy(
            src_ref=hid.at[k, pl.ds(0, q - 1)], dst_ref=hid.at[k, pl.ds(0, q - 1)],
            send_sem=csend.at[k], recv_sem=crecv.at[k],
            device_id={"section": (sec + 1) % q}, device_id_type=MESH)

    def finish(k):
        c_all(k).wait_recv()
        res = jnp.dot(hid[k, 0], wout[:cols, :], preferred_element_type=F32)
        for j in range(1, q):
            res = res + jnp.dot(hid[k, j], wout[j * cols:(j + 1) * cols, :], preferred_element_type=F32)

        @pl.when(k == 0)
        def _():
            back[0] = res.astype(BF16)

        @pl.when(k != 0)
        def _():
            osend[k] = res.astype(BF16)
            d_copy(k).start()

    def stage(i, c):
        @pl.when(i < n)
        def _():
            project((n - i) % n)

        @pl.when((i >= 1) & (i <= n))
        def _():
            activate((n - i + 1) % n)

        @pl.when(i >= 2)
        def _():
            finish((n - i + 2) % n)

        return c

    lax.fori_loop(0, n + 2, stage, 0)

    acc[...] = jnp.zeros_like(acc)

    def combine(i, c):
        k = (n - i) % n
        d = partner(me, k, n)

        @pl.when(k != 0)
        def _():
            d_copy(k).wait_recv()

        w = jnp.where(code[d] == slot_iota, wts[d], 0.0)
        upper = w.astype(BF16)
        lower = (w - upper.astype(F32)).astype(BF16)
        dims = (((0,), (0,)), ((), ()))
        acc[...] += lax.dot_general(upper, back[k], dims, preferred_element_type=F32) + lax.dot_general(
            lower, back[k], dims, preferred_element_type=F32)
        return c

    lax.fori_loop(0, n, combine, 0)
    out[...] = acc[...].astype(out.dtype)

    def drain(k, c):
        @pl.when(k != 0)
        def _():
            a_copy(k).wait_send()
            d_copy(k).wait_send()

        b_all(k).wait_send()
        c_all(k).wait_send()
        return c

    lax.fori_loop(0, n, drain, 0)


def exchanged(tokens, gate_up, down_weight, expert_ids, gate_values, owner_map):
    tok_rows = tokens.shape[0]
    experts = lax.axis_size("expert")
    slot_count = max(2, 3 * tok_rows * expert_ids.shape[1] // (8 * experts))
    device_ids = jnp.arange(experts, dtype=jnp.int32)
    named = (expert_ids[:, :, None] == device_ids[None, None, :]).astype(jnp.float32)
    placed = (owner_map[:, None] == device_ids[None, :]).astype(jnp.float32)
    routed = jnp.einsum("tjk,kd->tjd", named, placed)
    picked = jnp.sum(routed, axis=1)
    weighted = jnp.einsum("tj,tjd->td", gate_values, routed, precision=lax.Precision.HIGHEST)
    ranks = jnp.cumsum(picked, axis=0) - 1.0
    slot_hot = picked[:, :, None] * (
        ranks[:, :, None] == jnp.arange(slot_count, dtype=jnp.float32)[None, None, :]
    )
    slot_mask = slot_hot.astype(jnp.bfloat16)
    sending = jnp.einsum(
        "tdc,tf->dcf", slot_mask, tokens, preferred_element_type=jnp.float32
    ).astype(jnp.bfloat16)
    weight_in = gate_up[0]
    weight_out = down_weight[0]
    partial_sums = jnp.einsum(
        "scd,dgf->scgf",
        lax.all_to_all(sending, "expert", split_axis=0, concat_axis=0, tiled=True),
        weight_in,
        preferred_element_type=jnp.float32,
    )
    shares = lax.psum_scatter(
        partial_sums.astype(jnp.bfloat16), "section", scatter_dimension=0, tiled=True
    ).astype(jnp.float32)
    active = (jax.nn.silu(shares[:, :, 0]) * shares[:, :, 1]).astype(jnp.bfloat16)
    hidden = lax.all_gather(active, "section", axis=0, tiled=True)
    expert_out = jnp.einsum(
        "scf,fd->scd", hidden, weight_out, preferred_element_type=jnp.float32
    ).astype(jnp.bfloat16)
    arrived = lax.all_to_all(expert_out, "expert", split_axis=0, concat_axis=0, tiled=True)
    slot_weight = jnp.einsum("tdc,td->dc", slot_hot, weighted, precision=lax.Precision.HIGHEST)
    scaled = slot_weight[:, :, None] * arrived.astype(jnp.float32)
    upper_part = lax.optimization_barrier(scaled.astype(jnp.bfloat16))
    lower_part = (scaled - upper_part.astype(jnp.float32)).astype(jnp.bfloat16)
    mixed = jnp.einsum("tdc,dcf->tf", slot_mask, upper_part, preferred_element_type=jnp.float32)
    mixed = mixed + jnp.einsum(
        "tdc,dcf->tf", slot_mask, lower_part, preferred_element_type=jnp.float32
    )
    return mixed.astype(jnp.bfloat16)


def on_device(tokens, gate_up, down_weight, expert_ids, gate_values, owner_map):
    rows, width = tokens.shape
    top = expert_ids.shape[1]
    n, q = lax.axis_size("expert"), lax.axis_size("section")
    slots = max(2, 3 * rows * top // (8 * n))
    slots = -(-slots // 16) * 16
    hidden = down_weight.shape[1]
    cols = hidden // q
    if width % 128 or cols % 128 or n & (n - 1):
        return exchanged(tokens, gate_up, down_weight, expert_ids, gate_values, owner_map)

    owners = jnp.arange(n, dtype=jnp.int32)
    held = jnp.sum(jnp.where(owner_map[:, None] == owners[None, :], owners[:, None], 0), axis=0)
    hits = expert_ids.T[None, :, :] == held[:, None, None]
    picked = jnp.any(hits, axis=1)
    weights = jnp.sum(jnp.where(hits, gate_values.T[None, :, :], 0.0), axis=1)
    upto = (jnp.arange(rows)[:, None] <= jnp.arange(rows)[None, :]).astype(BF16)
    ranks = jnp.dot(picked.astype(BF16), upto, preferred_element_type=F32).astype(jnp.int32) - 1
    code = jnp.where(picked, ranks, -1)[:, None, :]
    weights = weights[:, None, :]
    weight_in = jnp.swapaxes(gate_up[0], 0, 1)

    vmem = pl.BlockSpec(memory_space=pltpu.VMEM)
    hbm = pl.BlockSpec(memory_space=pl.ANY)
    dma = pltpu.SemaphoreType.DMA
    return pl.pallas_call(
        functools.partial(layer_kernel, n, q),
        out_shape=jax.ShapeDtypeStruct((rows, width), BF16),
        in_specs=[vmem, vmem, vmem, hbm, hbm],
        out_specs=vmem,
        scratch_shapes=[
            pltpu.VMEM((2, width, hidden), BF16),
            pltpu.VMEM((hidden, width), BF16),
            pltpu.VMEM((n, slots, width), BF16),
            pltpu.VMEM((n, slots, width), BF16),
            pltpu.VMEM((n, q, slots, 2 * cols), BF16),
            pltpu.VMEM((n, q - 1, slots, 2 * cols), BF16),
            pltpu.VMEM((n, q, slots, cols), BF16),
            pltpu.VMEM((n, slots, width), BF16),
            pltpu.VMEM((n, slots, width), BF16),
            pltpu.VMEM((rows, width), F32),
            dma((2,)),
            dma((n,)), dma((n,)), dma((n,)), dma((n,)), dma((n,)), dma((n,)), dma((n,)), dma((n,)),
        ],
        compiler_params=pltpu.CompilerParams(
            collective_id=0, has_side_effects=True, vmem_limit_bytes=60 * 1024 * 1024
        ),
    )(tokens, code, weights, weight_in, down_weight[0])


def solution(mesh):
    placed = (
        P("expert", "section"),
        P("expert", "section", None, None),
        P("expert", None, "section"),
        P("expert", None),
        P("expert", None),
        P(),
    )
    return jax.shard_map(
        on_device, mesh=mesh, in_specs=placed, out_specs=P("expert", "section"), check_vma=False
    )
```

```python
import functools

import jax
import jax.numpy as jnp
from jax import lax
from jax.experimental import pallas as pl
from jax.experimental.pallas import tpu as pltpu
from jax.sharding import PartitionSpec as P

MESH = pl.DeviceIdType.MESH
F32, BF16 = jnp.float32, jnp.bfloat16


def partner(me, k, n):
    out, bit = me, 1
    while bit < n:
        out = out + ((k // bit) % 2) * (1 - 2 * ((me // bit) % 2)) * bit
        bit *= 2
    return out


def layer_kernel(
    n, q,
    tok, ids, gates, owner, win_hbm, wout_hbm, out,
    raw, win, wout, send, recv, psend, precv, hid, osend, back, acc, code, wts,
    wsem, asend, arecv, bsend, brecv, csend, crecv, dsend, drecv,
):
    me = lax.axis_index("expert")
    sec = lax.axis_index("section")
    slots, width = send.shape[1], send.shape[2]
    rows = tok.shape[0]
    cols = hid.shape[3]

    load_in = pltpu.make_async_copy(win_hbm, raw, wsem.at[0])
    load_out = pltpu.make_async_copy(wout_hbm, wout, wsem.at[1])
    load_in.start()
    load_out.start()

    barrier = pltpu.get_barrier_semaphore()

    def greet(k, c):
        pl.semaphore_signal(barrier, inc=1, device_id={"expert": partner(me, k, n)}, device_id_type=MESH)
        return c

    lax.fori_loop(1, n, greet, 0)
    for r in range(1, q):
        pl.semaphore_signal(barrier, inc=1, device_id={"section": (sec + r) % q}, device_id_type=MESH)

    def find(d, c):
        held = jnp.int32(0)
        for k in range(n):
            held = held + jnp.where(owner[k] == d, k, 0)
        hit = ids[...] == held
        code[pl.ds(d, 1), :] = jnp.max(jnp.where(hit, 1, 0), axis=0, keepdims=True)
        wts[pl.ds(d, 1), :] = jnp.sum(jnp.where(hit, gates[...], 0.0), axis=0, keepdims=True)
        return c

    lax.fori_loop(0, n, find, 0)
    upto = lax.broadcasted_iota(jnp.int32, (rows, rows), 0) <= lax.broadcasted_iota(jnp.int32, (rows, rows), 1)
    ranks = jnp.dot(
        code[...].astype(F32).astype(BF16), jnp.where(upto, 1.0, 0.0).astype(BF16), preferred_element_type=F32)
    code[...] = jnp.where(code[...] > 0, ranks.astype(jnp.int32) - 1, -1)
    pl.semaphore_wait(barrier, n + q - 2)

    slot_iota = lax.broadcasted_iota(jnp.int32, (slots, rows), 0)

    def a_copy(k):
        return pltpu.make_async_remote_copy(
            src_ref=send.at[k], dst_ref=recv.at[k], send_sem=asend.at[k], recv_sem=arecv.at[k],
            device_id={"expert": partner(me, k, n)}, device_id_type=MESH)

    def d_copy(k):
        return pltpu.make_async_remote_copy(
            src_ref=osend.at[k], dst_ref=back.at[k], send_sem=dsend.at[k], recv_sem=drecv.at[k],
            device_id={"expert": partner(me, k, n)}, device_id_type=MESH)

    def pick(k):
        hot = (code[pl.ds(partner(me, k, n), 1), :] == slot_iota).astype(F32).astype(BF16)
        return jnp.dot(hot, tok[...], preferred_element_type=F32).astype(BF16)

    def dispatch(i, c):
        k = n - i
        send[k] = pick(k)
        a_copy(k).start()
        return c

    lax.fori_loop(1, n, dispatch, 0)
    recv[0] = pick(0)
    load_in.wait()

    def split(i, c):
        part = pl.ds(pl.multiple_of(i * 128, 128), 128)
        win[0, part, :] = raw[part, 0, :]
        win[1, part, :] = raw[part, 1, :]
        return c

    lax.fori_loop(0, width // 128, split, 0)
    load_out.wait()

    def project(k):
        @pl.when(k != 0)
        def _():
            a_copy(k).wait_recv()

        for step in range(q):
            r = (step + 1) % q
            j = (sec + r) % q
            at = pl.ds(pl.multiple_of(j * cols, cols), cols)
            for g in range(2):
                part = jnp.dot(recv[k], win[g, :, at], preferred_element_type=F32)
                psend[k, r, :, g * cols:(g + 1) * cols] = part.astype(BF16)
            if r:
                pltpu.make_async_remote_copy(
                    src_ref=psend.at[k, r], dst_ref=precv.at[k, r - 1],
                    send_sem=bsend.at[k], recv_sem=brecv.at[k],
                    device_id={"section": j}, device_id_type=MESH).start()

    def b_all(k):
        return pltpu.make_async_remote_copy(
            src_ref=psend.at[k, pl.ds(1, q - 1)], dst_ref=precv.at[k],
            send_sem=bsend.at[k], recv_sem=brecv.at[k],
            device_id={"section": (sec + 1) % q}, device_id_type=MESH)

    def activate(k):
        b_all(k).wait_recv()
        total = psend[k, 0].astype(F32)
        for r in range(q - 1):
            total = total + precv[k, r].astype(F32)
        gate, up = total[:, :cols], total[:, cols:]
        hid[k, sec] = (gate / (1.0 + jnp.exp(-gate)) * up).astype(BF16)
        for r in range(1, q):
            pltpu.make_async_remote_copy(
                src_ref=hid.at[k, sec], dst_ref=hid.at[k, sec],
                send_sem=csend.at[k], recv_sem=crecv.at[k],
                device_id={"section": (sec + r) % q}, device_id_type=MESH).start()

    def c_all(k):
        return pltpu.make_async_remote_copy(
            src_ref=hid.at[k, pl.ds(0, q - 1)], dst_ref=hid.at[k, pl.ds(0, q - 1)],
            send_sem=csend.at[k], recv_sem=crecv.at[k],
            device_id={"section": (sec + 1) % q}, device_id_type=MESH)

    def finish(k):
        c_all(k).wait_recv()
        res = jnp.dot(hid[k, 0], wout[:cols, :], preferred_element_type=F32)
        for j in range(1, q):
            res = res + jnp.dot(hid[k, j], wout[j * cols:(j + 1) * cols, :], preferred_element_type=F32)

        @pl.when(k == 0)
        def _():
            back[0] = res.astype(BF16)

        @pl.when(k != 0)
        def _():
            osend[k] = res.astype(BF16)
            d_copy(k).start()

    def stage(i, c):
        @pl.when(i < n)
        def _():
            project((n - i) % n)

        @pl.when((i >= 1) & (i <= n))
        def _():
            activate((n - i + 1) % n)

        @pl.when(i >= 2)
        def _():
            finish((n - i + 2) % n)

        return c

    lax.fori_loop(0, n + 2, stage, 0)

    acc[...] = jnp.zeros_like(acc)

    def combine(i, c):
        k = (n - i) % n
        d = partner(me, k, n)

        @pl.when(k != 0)
        def _():
            d_copy(k).wait_recv()

        w = jnp.where(code[pl.ds(d, 1), :] == slot_iota, wts[pl.ds(d, 1), :], 0.0)
        upper = w.astype(BF16)
        lower = (w - upper.astype(F32)).astype(BF16)
        dims = (((0,), (0,)), ((), ()))
        acc[...] += lax.dot_general(upper, back[k], dims, preferred_element_type=F32) + lax.dot_general(
            lower, back[k], dims, preferred_element_type=F32)
        return c

    lax.fori_loop(0, n, combine, 0)
    out[...] = acc[...].astype(out.dtype)

    def drain(k, c):
        @pl.when(k != 0)
        def _():
            a_copy(k).wait_send()
            d_copy(k).wait_send()

        b_all(k).wait_send()
        c_all(k).wait_send()
        return c

    lax.fori_loop(0, n, drain, 0)


def exchanged(tokens, gate_up, down_weight, expert_ids, gate_values, owner_map):
    tok_rows = tokens.shape[0]
    experts = lax.axis_size("expert")
    slot_count = max(2, 3 * tok_rows * expert_ids.shape[1] // (8 * experts))
    device_ids = jnp.arange(experts, dtype=jnp.int32)
    named = (expert_ids[:, :, None] == device_ids[None, None, :]).astype(jnp.float32)
    placed = (owner_map[:, None] == device_ids[None, :]).astype(jnp.float32)
    routed = jnp.einsum("tjk,kd->tjd", named, placed)
    picked = jnp.sum(routed, axis=1)
    weighted = jnp.einsum("tj,tjd->td", gate_values, routed, precision=lax.Precision.HIGHEST)
    ranks = jnp.cumsum(picked, axis=0) - 1.0
    slot_hot = picked[:, :, None] * (
        ranks[:, :, None] == jnp.arange(slot_count, dtype=jnp.float32)[None, None, :]
    )
    slot_mask = slot_hot.astype(jnp.bfloat16)
    sending = jnp.einsum(
        "tdc,tf->dcf", slot_mask, tokens, preferred_element_type=jnp.float32
    ).astype(jnp.bfloat16)
    weight_in = gate_up[0]
    weight_out = down_weight[0]
    partial_sums = jnp.einsum(
        "scd,dgf->scgf",
        lax.all_to_all(sending, "expert", split_axis=0, concat_axis=0, tiled=True),
        weight_in,
        preferred_element_type=jnp.float32,
    )
    shares = lax.psum_scatter(
        partial_sums.astype(jnp.bfloat16), "section", scatter_dimension=0, tiled=True
    ).astype(jnp.float32)
    active = (jax.nn.silu(shares[:, :, 0]) * shares[:, :, 1]).astype(jnp.bfloat16)
    hidden = lax.all_gather(active, "section", axis=0, tiled=True)
    expert_out = jnp.einsum(
        "scf,fd->scd", hidden, weight_out, preferred_element_type=jnp.float32
    ).astype(jnp.bfloat16)
    arrived = lax.all_to_all(expert_out, "expert", split_axis=0, concat_axis=0, tiled=True)
    slot_weight = jnp.einsum("tdc,td->dc", slot_hot, weighted, precision=lax.Precision.HIGHEST)
    scaled = slot_weight[:, :, None] * arrived.astype(jnp.float32)
    upper_part = lax.optimization_barrier(scaled.astype(jnp.bfloat16))
    lower_part = (scaled - upper_part.astype(jnp.float32)).astype(jnp.bfloat16)
    mixed = jnp.einsum("tdc,dcf->tf", slot_mask, upper_part, preferred_element_type=jnp.float32)
    mixed = mixed + jnp.einsum(
        "tdc,dcf->tf", slot_mask, lower_part, preferred_element_type=jnp.float32
    )
    return mixed.astype(jnp.bfloat16)


def on_device(tokens, gate_up, down_weight, expert_ids, gate_values, owner_map):
    rows, width = tokens.shape
    top = expert_ids.shape[1]
    n, q = lax.axis_size("expert"), lax.axis_size("section")
    slots = max(2, 3 * rows * top // (8 * n))
    slots = -(-slots // 16) * 16
    hidden = down_weight.shape[1]
    cols = hidden // q
    if width % 128 or cols % 128 or n & (n - 1):
        return exchanged(tokens, gate_up, down_weight, expert_ids, gate_values, owner_map)

    weight_in = gate_up[0]

    vmem = pl.BlockSpec(memory_space=pltpu.VMEM)
    hbm = pl.BlockSpec(memory_space=pl.ANY)
    dma = pltpu.SemaphoreType.DMA
    return pl.pallas_call(
        functools.partial(layer_kernel, n, q),
        out_shape=jax.ShapeDtypeStruct((rows, width), BF16),
        in_specs=[vmem, vmem, vmem, pl.BlockSpec(memory_space=pltpu.SMEM), hbm, hbm],
        out_specs=vmem,
        scratch_shapes=[
            pltpu.VMEM((width, 2, hidden), BF16),
            pltpu.VMEM((2, width, hidden), BF16),
            pltpu.VMEM((hidden, width), BF16),
            pltpu.VMEM((n, slots, width), BF16),
            pltpu.VMEM((n, slots, width), BF16),
            pltpu.VMEM((n, q, slots, 2 * cols), BF16),
            pltpu.VMEM((n, q - 1, slots, 2 * cols), BF16),
            pltpu.VMEM((n, q, slots, cols), BF16),
            pltpu.VMEM((n, slots, width), BF16),
            pltpu.VMEM((n, slots, width), BF16),
            pltpu.VMEM((rows, width), F32),
            pltpu.VMEM((n, rows), jnp.int32),
            pltpu.VMEM((n, rows), F32),
            dma((2,)),
            dma((n,)), dma((n,)), dma((n,)), dma((n,)), dma((n,)), dma((n,)), dma((n,)), dma((n,)),
        ],
        compiler_params=pltpu.CompilerParams(
            collective_id=0, has_side_effects=True, vmem_limit_bytes=60 * 1024 * 1024
        ),
    )(tokens, expert_ids.T, gate_values.T, owner_map, weight_in, down_weight[0])


def solution(mesh):
    placed = (
        P("expert", "section"),
        P("expert", "section", None, None),
        P("expert", None, "section"),
        P("expert", None),
        P("expert", None),
        P(),
    )
    return jax.shard_map(
        on_device, mesh=mesh, in_specs=placed, out_specs=P("expert", "section"), check_vma=False
    )
```

```python
import functools

import jax
import jax.numpy as jnp
from jax import lax
from jax.experimental import pallas as pl
from jax.experimental.pallas import tpu as pltpu
from jax.sharding import PartitionSpec as P

MESH = pl.DeviceIdType.MESH
F32, BF16 = jnp.float32, jnp.bfloat16


def partner(me, k, n):
    out, bit = me, 1
    while bit < n:
        out = out + ((k // bit) % 2) * (1 - 2 * ((me // bit) % 2)) * bit
        bit *= 2
    return out


def layer_kernel(
    n, q,
    tok, ids, gates, owner, win_hbm, wout_hbm, out,
    raw, win, wout, send, recv, far, psend, precv, hid, osend, back, sums, met, acc, code, wts, table, mixer,
    wsem, tsend, trecv, fsend, frecv, asend, arecv, bsend, brecv, csend, crecv, dsend, drecv, gsend, grecv,
):
    me = lax.axis_index("expert")
    sec = lax.axis_index("section")
    half = n // 2
    slots = send.shape[1]
    rows, width = tok.shape
    cols = hid.shape[3]
    pieces, piece = far.shape[0], far.shape[2]

    load_in = pltpu.make_async_copy(win_hbm, raw, wsem.at[0])
    load_out = pltpu.make_async_copy(wout_hbm, wout, wsem.at[1])
    load_in.start()
    load_out.start()

    barrier = pltpu.get_barrier_semaphore()

    def greet(k, c):
        pl.semaphore_signal(barrier, inc=1, device_id={"expert": partner(me, k, n)}, device_id_type=MESH)
        return c

    lax.fori_loop(1, half + 1, greet, 0)
    for r in range(1, q):
        pl.semaphore_signal(barrier, inc=1, device_id={"section": (sec + r) % q}, device_id_type=MESH)

    def find(d, c):
        held = jnp.int32(0)
        for k in range(n):
            held = held + jnp.where(owner[k] == d, k, 0)
        hit = ids[...] == held
        code[0, pl.ds(d, 1), :] = jnp.max(jnp.where(hit, 1, 0), axis=0, keepdims=True)
        wts[0, pl.ds(d, 1), :] = jnp.sum(jnp.where(hit, gates[...], 0.0), axis=0, keepdims=True)
        return c

    lax.fori_loop(0, n, find, 0)
    upto = lax.broadcasted_iota(jnp.int32, (rows, rows), 0) <= lax.broadcasted_iota(jnp.int32, (rows, rows), 1)
    ranks = jnp.dot(
        code[0].astype(F32).astype(BF16), jnp.where(upto, 1.0, 0.0).astype(BF16), preferred_element_type=F32)
    code[0] = jnp.where(code[0] > 0, ranks.astype(jnp.int32) - 1, -1)
    pl.semaphore_wait(barrier, half + q - 1)

    slot_iota = lax.broadcasted_iota(jnp.int32, (slots, rows), 0)
    across = {"expert": partner(me, half, n)}

    def span(p):
        return pl.ds(pl.multiple_of(p * piece, piece), piece)

    def t_copy(ref, i):
        return pltpu.make_async_remote_copy(
            src_ref=ref.at[0], dst_ref=ref.at[1], send_sem=tsend.at[i], recv_sem=trecv.at[i],
            device_id=across, device_id_type=MESH)

    def f_copy(p):
        return pltpu.make_async_remote_copy(
            src_ref=tok.at[:, span(p)], dst_ref=far.at[p], send_sem=fsend.at[p], recv_sem=frecv.at[p],
            device_id=across, device_id_type=MESH)

    def a_copy(k):
        return pltpu.make_async_remote_copy(
            src_ref=send.at[k], dst_ref=recv.at[k], send_sem=asend.at[k], recv_sem=arecv.at[k],
            device_id={"expert": partner(me, k % half, n)}, device_id_type=MESH)

    def a_part(k, p):
        return pltpu.make_async_remote_copy(
            src_ref=send.at[k, :, span(p)], dst_ref=recv.at[k, :, span(p)],
            send_sem=asend.at[k], recv_sem=arecv.at[k],
            device_id={"expert": partner(me, k % half, n)}, device_id_type=MESH)

    def d_copy(k):
        return pltpu.make_async_remote_copy(
            src_ref=osend.at[k], dst_ref=back.at[k], send_sem=dsend.at[k], recv_sem=drecv.at[k],
            device_id={"expert": partner(me, k % half, n)}, device_id_type=MESH)

    def g_copy(p):
        return pltpu.make_async_remote_copy(
            src_ref=sums.at[p], dst_ref=met.at[p], send_sem=gsend.at[p], recv_sem=grecv.at[p],
            device_id=across, device_id_type=MESH)

    t_copy(code, 0).start()
    t_copy(wts, 1).start()

    def hot(side, k):
        return (code[side, pl.ds(partner(me, k, n), 1), :] == slot_iota).astype(F32).astype(BF16)

    def dispatch(i, c):
        k = half - i
        send[k] = jnp.dot(hot(0, k), tok[...], preferred_element_type=F32).astype(BF16)
        a_copy(k).start()
        return c

    lax.fori_loop(1, half, dispatch, 0)

    def cross(p, c):
        f_copy(p).start()
        return c

    lax.fori_loop(0, pieces, cross, 0)
    recv[0] = jnp.dot(hot(0, 0), tok[...], preferred_element_type=F32).astype(BF16)
    load_in.wait()

    def split(i, c):
        part = pl.ds(pl.multiple_of(i * 128, 128), 128)
        win[0, part, :] = raw[part, 0, :]
        win[1, part, :] = raw[part, 1, :]
        return c

    lax.fori_loop(0, width // 128, split, 0)
    load_out.wait()
    t_copy(code, 0).wait_recv()
    t_copy(wts, 1).wait_recv()

    def weigh(side):
        def one(k, c):
            at = pl.ds(partner(me, k, n), 1)
            table[pl.ds(pl.multiple_of(k * slots, 16), slots), :] = jnp.where(
                code[side, at, :] == slot_iota, wts[side, at, :], 0.0)
            return c

        lax.fori_loop(0, half, one, 0)
        turned = table[...].T
        upper = turned.astype(BF16)
        mixer[side, 0] = upper
        mixer[side, 1] = (turned - upper.astype(F32)).astype(BF16)

    weigh(0)
    weigh(1)

    def relay(p):
        f_copy(p).wait_recv()
        block = far[p]
        recv[half, :, span(p)] = jnp.dot(hot(1, 0), block, preferred_element_type=F32).astype(BF16)

        def one(k, c):
            send[half + k, :, span(p)] = jnp.dot(hot(1, k), block, preferred_element_type=F32).astype(BF16)
            a_part(half + k, p).start()
            return c

        lax.fori_loop(1, half, one, 0)

    def project(k):
        @pl.when(k % half != 0)
        def _():
            a_copy(k).wait_recv()

        for step in range(q):
            r = (step + 1) % q
            j = (sec + r) % q
            at = pl.ds(pl.multiple_of(j * cols, cols), cols)
            for g in range(2):
                part = jnp.dot(recv[k], win[g, :, at], preferred_element_type=F32)
                psend[k, r, :, g * cols:(g + 1) * cols] = part.astype(BF16)
            if r:
                pltpu.make_async_remote_copy(
                    src_ref=psend.at[k, r], dst_ref=precv.at[k, r - 1],
                    send_sem=bsend.at[k], recv_sem=brecv.at[k],
                    device_id={"section": j}, device_id_type=MESH).start()

    def b_all(k):
        return pltpu.make_async_remote_copy(
            src_ref=psend.at[k, pl.ds(1, q - 1)], dst_ref=precv.at[k],
            send_sem=bsend.at[k], recv_sem=brecv.at[k],
            device_id={"section": (sec + 1) % q}, device_id_type=MESH)

    def activate(k):
        b_all(k).wait_recv()
        total = psend[k, 0].astype(F32)
        for r in range(q - 1):
            total = total + precv[k, r].astype(F32)
        gate, up = total[:, :cols], total[:, cols:]
        hid[k, sec] = (gate / (1.0 + jnp.exp(-gate)) * up).astype(BF16)
        for r in range(1, q):
            pltpu.make_async_remote_copy(
                src_ref=hid.at[k, sec], dst_ref=hid.at[k, sec],
                send_sem=csend.at[k], recv_sem=crecv.at[k],
                device_id={"section": (sec + r) % q}, device_id_type=MESH).start()

    def c_all(k):
        return pltpu.make_async_remote_copy(
            src_ref=hid.at[k, pl.ds(0, q - 1)], dst_ref=hid.at[k, pl.ds(0, q - 1)],
            send_sem=csend.at[k], recv_sem=crecv.at[k],
            device_id={"section": (sec + 1) % q}, device_id_type=MESH)

    def finish(k):
        c_all(k).wait_recv()
        res = jnp.dot(hid[k, 0], wout[:cols, :], preferred_element_type=F32)
        for j in range(1, q):
            res = res + jnp.dot(hid[k, j], wout[j * cols:(j + 1) * cols, :], preferred_element_type=F32)

        @pl.when(k % half == 0)
        def _():
            back[k] = res.astype(BF16)

        @pl.when(k % half != 0)
        def _():
            osend[k] = res.astype(BF16)
            d_copy(k).start()

    def early(i, c):
        project(i)

        def some(p, e):
            relay(p)
            return e

        lax.fori_loop(i * pieces // half, (i + 1) * pieces // half, some, 0)

        @pl.when(i >= 1)
        def _():
            activate(i - 1)

        @pl.when(i >= 2)
        def _():
            finish(i - 2)

        return c

    def late(i, c):
        @pl.when(i < n)
        def _():
            project(i)

        @pl.when(i <= n)
        def _():
            activate(i - 1)

        finish(i - 2)
        return c

    lax.fori_loop(0, half, early, 0)
    lax.fori_loop(half, n + 2, late, 0)

    def arrived(first):
        def one(k, c):
            d_copy(first + k).wait_recv()
            return c

        lax.fori_loop(1, half, one, 0)

    def mixed(side, p):
        rhs = back[pl.ds(side * half, half), :, span(p)].reshape(half * slots, piece)
        return jnp.dot(mixer[side, 0], rhs, preferred_element_type=F32) + jnp.dot(
            mixer[side, 1], rhs, preferred_element_type=F32)

    arrived(half)

    def give(p, c):
        sums[p] = mixed(1, p).astype(BF16)
        g_copy(p).start()
        return c

    lax.fori_loop(0, pieces, give, 0)
    arrived(0)

    def own(p, c):
        acc[p] = mixed(0, p)
        return c

    lax.fori_loop(0, pieces, own, 0)

    def close(p, c):
        g_copy(p).wait_recv()
        out[:, span(p)] = (acc[p] + met[p].astype(F32)).astype(out.dtype)
        return c

    lax.fori_loop(0, pieces, close, 0)

    def drain(k, c):
        @pl.when(k % half != 0)
        def _():
            a_copy(k).wait_send()
            d_copy(k).wait_send()

        b_all(k).wait_send()
        c_all(k).wait_send()
        return c

    lax.fori_loop(0, n, drain, 0)

    def drain_pieces(p, c):
        f_copy(p).wait_send()
        g_copy(p).wait_send()
        return c

    lax.fori_loop(0, pieces, drain_pieces, 0)
    t_copy(code, 0).wait_send()
    t_copy(wts, 1).wait_send()


def exchanged(tokens, gate_up, down_weight, expert_ids, gate_values, owner_map):
    tok_rows = tokens.shape[0]
    experts = lax.axis_size("expert")
    slot_count = max(2, 3 * tok_rows * expert_ids.shape[1] // (8 * experts))
    device_ids = jnp.arange(experts, dtype=jnp.int32)
    named = (expert_ids[:, :, None] == device_ids[None, None, :]).astype(jnp.float32)
    placed = (owner_map[:, None] == device_ids[None, :]).astype(jnp.float32)
    routed = jnp.einsum("tjk,kd->tjd", named, placed)
    picked = jnp.sum(routed, axis=1)
    weighted = jnp.einsum("tj,tjd->td", gate_values, routed, precision=lax.Precision.HIGHEST)
    ranks = jnp.cumsum(picked, axis=0) - 1.0
    slot_hot = picked[:, :, None] * (
        ranks[:, :, None] == jnp.arange(slot_count, dtype=jnp.float32)[None, None, :]
    )
    slot_mask = slot_hot.astype(jnp.bfloat16)
    sending = jnp.einsum(
        "tdc,tf->dcf", slot_mask, tokens, preferred_element_type=jnp.float32
    ).astype(jnp.bfloat16)
    weight_in = gate_up[0]
    weight_out = down_weight[0]
    partial_sums = jnp.einsum(
        "scd,dgf->scgf",
        lax.all_to_all(sending, "expert", split_axis=0, concat_axis=0, tiled=True),
        weight_in,
        preferred_element_type=jnp.float32,
    )
    shares = lax.psum_scatter(
        partial_sums.astype(jnp.bfloat16), "section", scatter_dimension=0, tiled=True
    ).astype(jnp.float32)
    active = (jax.nn.silu(shares[:, :, 0]) * shares[:, :, 1]).astype(jnp.bfloat16)
    hidden = lax.all_gather(active, "section", axis=0, tiled=True)
    expert_out = jnp.einsum(
        "scf,fd->scd", hidden, weight_out, preferred_element_type=jnp.float32
    ).astype(jnp.bfloat16)
    arrived = lax.all_to_all(expert_out, "expert", split_axis=0, concat_axis=0, tiled=True)
    slot_weight = jnp.einsum("tdc,td->dc", slot_hot, weighted, precision=lax.Precision.HIGHEST)
    scaled = slot_weight[:, :, None] * arrived.astype(jnp.float32)
    upper_part = lax.optimization_barrier(scaled.astype(jnp.bfloat16))
    lower_part = (scaled - upper_part.astype(jnp.float32)).astype(jnp.bfloat16)
    mixed = jnp.einsum("tdc,dcf->tf", slot_mask, upper_part, preferred_element_type=jnp.float32)
    mixed = mixed + jnp.einsum(
        "tdc,dcf->tf", slot_mask, lower_part, preferred_element_type=jnp.float32
    )
    return mixed.astype(jnp.bfloat16)


def on_device(tokens, gate_up, down_weight, expert_ids, gate_values, owner_map):
    rows, width = tokens.shape
    top = expert_ids.shape[1]
    n, q = lax.axis_size("expert"), lax.axis_size("section")
    slots = max(2, 3 * rows * top // (8 * n))
    slots = -(-slots // 16) * 16
    hidden = down_weight.shape[1]
    cols = hidden // q
    if width % 128 or cols % 128 or n < 4 or n & (n - 1):
        return exchanged(tokens, gate_up, down_weight, expert_ids, gate_values, owner_map)

    weight_in = gate_up[0]
    half = n // 2
    piece = 256 if width % 256 == 0 else 128
    pieces = width // piece

    vmem = pl.BlockSpec(memory_space=pltpu.VMEM)
    hbm = pl.BlockSpec(memory_space=pl.ANY)
    dma = pltpu.SemaphoreType.DMA
    return pl.pallas_call(
        functools.partial(layer_kernel, n, q),
        out_shape=jax.ShapeDtypeStruct((rows, width), BF16),
        in_specs=[vmem, vmem, vmem, pl.BlockSpec(memory_space=pltpu.SMEM), hbm, hbm],
        out_specs=vmem,
        scratch_shapes=[
            pltpu.VMEM((width, 2, hidden), BF16),
            pltpu.VMEM((2, width, hidden), BF16),
            pltpu.VMEM((hidden, width), BF16),
            pltpu.VMEM((n, slots, width), BF16),
            pltpu.VMEM((n, slots, width), BF16),
            pltpu.VMEM((pieces, rows, piece), BF16),
            pltpu.VMEM((n, q, slots, 2 * cols), BF16),
            pltpu.VMEM((n, q - 1, slots, 2 * cols), BF16),
            pltpu.VMEM((n, q, slots, cols), BF16),
            pltpu.VMEM((n, slots, width), BF16),
            pltpu.VMEM((n, slots, width), BF16),
            pltpu.VMEM((pieces, rows, piece), BF16),
            pltpu.VMEM((pieces, rows, piece), BF16),
            pltpu.VMEM((pieces, rows, piece), F32),
            pltpu.VMEM((2, n, rows), jnp.int32),
            pltpu.VMEM((2, n, rows), F32),
            pltpu.VMEM((half * slots, rows), F32),
            pltpu.VMEM((2, 2, rows, half * slots), BF16),
            dma((2,)), dma((2,)), dma((2,)), dma((pieces,)), dma((pieces,)),
            dma((n,)), dma((n,)), dma((n,)), dma((n,)), dma((n,)), dma((n,)), dma((n,)), dma((n,)),
            dma((pieces,)), dma((pieces,)),
        ],
        compiler_params=pltpu.CompilerParams(
            collective_id=0, has_side_effects=True, vmem_limit_bytes=60 * 1024 * 1024
        ),
    )(tokens, expert_ids.T, gate_values.T, owner_map, weight_in, down_weight[0])


def solution(mesh):
    placed = (
        P("expert", "section"),
        P("expert", "section", None, None),
        P("expert", None, "section"),
        P("expert", None),
        P("expert", None),
        P(),
    )
    return jax.shard_map(
        on_device, mesh=mesh, in_specs=placed, out_specs=P("expert", "section"), check_vma=False
    )
```

```python
import functools

import jax
import jax.numpy as jnp
from jax import lax
from jax.experimental import pallas as pl
from jax.experimental.pallas import tpu as pltpu
from jax.sharding import PartitionSpec as P

MESH = pl.DeviceIdType.MESH
F32, BF16 = jnp.float32, jnp.bfloat16


def partner(me, k, n):
    out, bit = me, 1
    while bit < n:
        out = out + ((k // bit) % 2) * (1 - 2 * ((me // bit) % 2)) * bit
        bit *= 2
    return out


def layer_kernel(
    n, q,
    tok, ids, gates, owner, win_hbm, wout_hbm, out,
    raw, win, wout, send, recv, psend, precv, hid, osend, back, acc, code, wts,
    wsem, asend, arecv, bsend, brecv, csend, crecv, dsend, drecv,
):
    me = lax.axis_index("expert")
    sec = lax.axis_index("section")
    slots, width = send.shape[1], send.shape[2]
    rows = tok.shape[0]
    cols = hid.shape[3]

    load_in = pltpu.make_async_copy(win_hbm, raw, wsem.at[0])
    load_out = pltpu.make_async_copy(wout_hbm, wout, wsem.at[1])
    load_in.start()
    load_out.start()

    barrier = pltpu.get_barrier_semaphore()

    def greet(k, c):
        pl.semaphore_signal(barrier, inc=1, device_id={"expert": partner(me, k, n)}, device_id_type=MESH)
        return c

    lax.fori_loop(1, n, greet, 0)
    for r in range(1, q):
        pl.semaphore_signal(barrier, inc=1, device_id={"section": (sec + r) % q}, device_id_type=MESH)

    def find(d, c):
        held = jnp.int32(0)
        for k in range(n):
            held = held + jnp.where(owner[k] == d, k, 0)
        hit = ids[...] == held
        code[pl.ds(d, 1), :] = jnp.max(jnp.where(hit, 1, 0), axis=0, keepdims=True)
        wts[pl.ds(d, 1), :] = jnp.sum(jnp.where(hit, gates[...], 0.0), axis=0, keepdims=True)
        return c

    lax.fori_loop(0, n, find, 0)
    upto = lax.broadcasted_iota(jnp.int32, (rows, rows), 0) <= lax.broadcasted_iota(jnp.int32, (rows, rows), 1)
    ranks = jnp.dot(
        code[...].astype(F32).astype(BF16), jnp.where(upto, 1.0, 0.0).astype(BF16), preferred_element_type=F32)
    code[...] = jnp.where(code[...] > 0, ranks.astype(jnp.int32) - 1, -1)
    pl.semaphore_wait(barrier, n + q - 2)

    slot_iota = lax.broadcasted_iota(jnp.int32, (slots, rows), 0)

    def a_copy(k):
        return pltpu.make_async_remote_copy(
            src_ref=send.at[k], dst_ref=recv.at[k], send_sem=asend.at[k], recv_sem=arecv.at[k],
            device_id={"expert": partner(me, k, n)}, device_id_type=MESH)

    def d_copy(k):
        return pltpu.make_async_remote_copy(
            src_ref=osend.at[k], dst_ref=back.at[k], send_sem=dsend.at[k], recv_sem=drecv.at[k],
            device_id={"expert": partner(me, k, n)}, device_id_type=MESH)

    def pick(k):
        hot = (code[pl.ds(partner(me, k, n), 1), :] == slot_iota).astype(F32).astype(BF16)
        return jnp.dot(hot, tok[...], preferred_element_type=F32).astype(BF16)

    def turn(i):
        half = n // 2
        return (i % 2) * (n - (i + 1) // 2) + (1 - i % 2) * ((half - i // 2) % half)

    def dispatch(i, c):
        k = turn(i)
        send[k] = pick(k)
        a_copy(k).start()
        return c

    lax.fori_loop(1, n, dispatch, 0)
    recv[0] = pick(0)
    load_in.wait()

    def split(i, c):
        part = pl.ds(pl.multiple_of(i * 128, 128), 128)
        win[0, part, :] = raw[part, 0, :]
        win[1, part, :] = raw[part, 1, :]
        return c

    lax.fori_loop(0, width // 128, split, 0)
    load_out.wait()

    def project(k):
        @pl.when(k != 0)
        def _():
            a_copy(k).wait_recv()

        for step in range(q):
            r = (step + 1) % q
            j = (sec + r) % q
            at = pl.ds(pl.multiple_of(j * cols, cols), cols)
            for g in range(2):
                part = jnp.dot(recv[k], win[g, :, at], preferred_element_type=F32)
                psend[k, r, :, g * cols:(g + 1) * cols] = part.astype(BF16)
            if r:
                pltpu.make_async_remote_copy(
                    src_ref=psend.at[k, r], dst_ref=precv.at[k, r - 1],
                    send_sem=bsend.at[k], recv_sem=brecv.at[k],
                    device_id={"section": j}, device_id_type=MESH).start()

    def b_all(k):
        return pltpu.make_async_remote_copy(
            src_ref=psend.at[k, pl.ds(1, q - 1)], dst_ref=precv.at[k],
            send_sem=bsend.at[k], recv_sem=brecv.at[k],
            device_id={"section": (sec + 1) % q}, device_id_type=MESH)

    def activate(k):
        b_all(k).wait_recv()
        total = psend[k, 0].astype(F32)
        for r in range(q - 1):
            total = total + precv[k, r].astype(F32)
        gate, up = total[:, :cols], total[:, cols:]
        hid[k, sec] = (gate / (1.0 + jnp.exp(-gate)) * up).astype(BF16)
        for r in range(1, q):
            pltpu.make_async_remote_copy(
                src_ref=hid.at[k, sec], dst_ref=hid.at[k, sec],
                send_sem=csend.at[k], recv_sem=crecv.at[k],
                device_id={"section": (sec + r) % q}, device_id_type=MESH).start()

    def c_all(k):
        return pltpu.make_async_remote_copy(
            src_ref=hid.at[k, pl.ds(0, q - 1)], dst_ref=hid.at[k, pl.ds(0, q - 1)],
            send_sem=csend.at[k], recv_sem=crecv.at[k],
            device_id={"section": (sec + 1) % q}, device_id_type=MESH)

    def finish(k):
        c_all(k).wait_recv()
        res = jnp.dot(hid[k, 0], wout[:cols, :], preferred_element_type=F32)
        for j in range(1, q):
            res = res + jnp.dot(hid[k, j], wout[j * cols:(j + 1) * cols, :], preferred_element_type=F32)

        @pl.when(k == 0)
        def _():
            back[0] = res.astype(BF16)

        @pl.when(k != 0)
        def _():
            osend[k] = res.astype(BF16)
            d_copy(k).start()

    def stage(i, c):
        @pl.when(i < n)
        def _():
            project(turn(i))

        @pl.when(i >= 2)
        def _():
            finish(turn(i - 2))

        @pl.when((i >= 1) & (i <= n))
        def _():
            activate(turn(i - 1))

        return c

    lax.fori_loop(0, n + 2, stage, 0)

    acc[...] = jnp.zeros_like(acc)

    def combine(i, c):
        k = (n - i) % n
        d = partner(me, k, n)

        @pl.when(k != 0)
        def _():
            d_copy(k).wait_recv()

        w = jnp.where(code[pl.ds(d, 1), :] == slot_iota, wts[pl.ds(d, 1), :], 0.0)
        upper = w.astype(BF16)
        lower = (w - upper.astype(F32)).astype(BF16)
        dims = (((0,), (0,)), ((), ()))
        acc[...] += lax.dot_general(upper, back[k], dims, preferred_element_type=F32) + lax.dot_general(
            lower, back[k], dims, preferred_element_type=F32)
        return c

    lax.fori_loop(0, n, combine, 0)
    out[...] = acc[...].astype(out.dtype)

    def drain(k, c):
        @pl.when(k != 0)
        def _():
            a_copy(k).wait_send()
            d_copy(k).wait_send()

        b_all(k).wait_send()
        c_all(k).wait_send()
        return c

    lax.fori_loop(0, n, drain, 0)


def exchanged(tokens, gate_up, down_weight, expert_ids, gate_values, owner_map):
    tok_rows = tokens.shape[0]
    experts = lax.axis_size("expert")
    slot_count = max(2, 3 * tok_rows * expert_ids.shape[1] // (8 * experts))
    device_ids = jnp.arange(experts, dtype=jnp.int32)
    named = (expert_ids[:, :, None] == device_ids[None, None, :]).astype(jnp.float32)
    placed = (owner_map[:, None] == device_ids[None, :]).astype(jnp.float32)
    routed = jnp.einsum("tjk,kd->tjd", named, placed)
    picked = jnp.sum(routed, axis=1)
    weighted = jnp.einsum("tj,tjd->td", gate_values, routed, precision=lax.Precision.HIGHEST)
    ranks = jnp.cumsum(picked, axis=0) - 1.0
    slot_hot = picked[:, :, None] * (
        ranks[:, :, None] == jnp.arange(slot_count, dtype=jnp.float32)[None, None, :]
    )
    slot_mask = slot_hot.astype(jnp.bfloat16)
    sending = jnp.einsum(
        "tdc,tf->dcf", slot_mask, tokens, preferred_element_type=jnp.float32
    ).astype(jnp.bfloat16)
    weight_in = gate_up[0]
    weight_out = down_weight[0]
    partial_sums = jnp.einsum(
        "scd,dgf->scgf",
        lax.all_to_all(sending, "expert", split_axis=0, concat_axis=0, tiled=True),
        weight_in,
        preferred_element_type=jnp.float32,
    )
    shares = lax.psum_scatter(
        partial_sums.astype(jnp.bfloat16), "section", scatter_dimension=0, tiled=True
    ).astype(jnp.float32)
    active = (jax.nn.silu(shares[:, :, 0]) * shares[:, :, 1]).astype(jnp.bfloat16)
    hidden = lax.all_gather(active, "section", axis=0, tiled=True)
    expert_out = jnp.einsum(
        "scf,fd->scd", hidden, weight_out, preferred_element_type=jnp.float32
    ).astype(jnp.bfloat16)
    arrived = lax.all_to_all(expert_out, "expert", split_axis=0, concat_axis=0, tiled=True)
    slot_weight = jnp.einsum("tdc,td->dc", slot_hot, weighted, precision=lax.Precision.HIGHEST)
    scaled = slot_weight[:, :, None] * arrived.astype(jnp.float32)
    upper_part = lax.optimization_barrier(scaled.astype(jnp.bfloat16))
    lower_part = (scaled - upper_part.astype(jnp.float32)).astype(jnp.bfloat16)
    mixed = jnp.einsum("tdc,dcf->tf", slot_mask, upper_part, preferred_element_type=jnp.float32)
    mixed = mixed + jnp.einsum(
        "tdc,dcf->tf", slot_mask, lower_part, preferred_element_type=jnp.float32
    )
    return mixed.astype(jnp.bfloat16)


def on_device(tokens, gate_up, down_weight, expert_ids, gate_values, owner_map):
    rows, width = tokens.shape
    top = expert_ids.shape[1]
    n, q = lax.axis_size("expert"), lax.axis_size("section")
    slots = max(2, 3 * rows * top // (8 * n))
    slots = -(-slots // 16) * 16
    hidden = down_weight.shape[1]
    cols = hidden // q
    if width % 128 or cols % 128 or n & (n - 1):
        return exchanged(tokens, gate_up, down_weight, expert_ids, gate_values, owner_map)

    weight_in = gate_up[0]

    vmem = pl.BlockSpec(memory_space=pltpu.VMEM)
    hbm = pl.BlockSpec(memory_space=pl.ANY)
    dma = pltpu.SemaphoreType.DMA
    return pl.pallas_call(
        functools.partial(layer_kernel, n, q),
        out_shape=jax.ShapeDtypeStruct((rows, width), BF16),
        in_specs=[vmem, vmem, vmem, pl.BlockSpec(memory_space=pltpu.SMEM), hbm, hbm],
        out_specs=vmem,
        scratch_shapes=[
            pltpu.VMEM((width, 2, hidden), BF16),
            pltpu.VMEM((2, width, hidden), BF16),
            pltpu.VMEM((hidden, width), BF16),
            pltpu.VMEM((n, slots, width), BF16),
            pltpu.VMEM((n, slots, width), BF16),
            pltpu.VMEM((n, q, slots, 2 * cols), BF16),
            pltpu.VMEM((n, q - 1, slots, 2 * cols), BF16),
            pltpu.VMEM((n, q, slots, cols), BF16),
            pltpu.VMEM((n, slots, width), BF16),
            pltpu.VMEM((n, slots, width), BF16),
            pltpu.VMEM((rows, width), F32),
            pltpu.VMEM((n, rows), jnp.int32),
            pltpu.VMEM((n, rows), F32),
            dma((2,)),
            dma((n,)), dma((n,)), dma((n,)), dma((n,)), dma((n,)), dma((n,)), dma((n,)), dma((n,)),
        ],
        compiler_params=pltpu.CompilerParams(
            collective_id=0, has_side_effects=True, vmem_limit_bytes=60 * 1024 * 1024
        ),
    )(tokens, expert_ids.T, gate_values.T, owner_map, weight_in, down_weight[0])


def solution(mesh):
    placed = (
        P("expert", "section"),
        P("expert", "section", None, None),
        P("expert", None, "section"),
        P("expert", None),
        P("expert", None),
        P(),
    )
    return jax.shard_map(
        on_device, mesh=mesh, in_specs=placed, out_specs=P("expert", "section"), check_vma=False
    )
```
